32 devices in a mesh: gx: 4 (over z), gy: 8 (over y, x, core).
Axes of the slice: x: 2, y: 2, z: 4, core: 2. Of those that a mesh axis runs over, the one named last changes fastest.
Arguments:
- data: bfloat16 [128, 512, 1024], P(None, 'gx', 'gy')
- inv_scale: float32 [128], replicated, may hold values from 0.1 to 1
- start: float32 [128, 32], replicated, may hold values from -6 to 6
- rank: int32 [1], replicated, may hold values from 24 to 32
Outputs:
- core: bfloat16 [32, 512, 1024], P(None, 'gx', 'gy')
- factor: float32 [128, 32], replicated
The draws below stay inside these ranges and needn't reach their ends.
Inputs may be any that keep to these rules, and one draw needn't show every extreme that they name: rank[0] is the number of leading columns of the factor that are kept.
All inputs are finite; a program needn't handle non-finite values.
Results may differ from the reference program's by a relative error of at most 0.0044.
Values sent between devices are 32-bit elements; how exact they have to be, the bound alone decides.
A program may use at most 64 MiB of HBM per device.

```python
import math
import jax
import jax.numpy as jnp
from jax import lax

V = 128
KMAX = 32
ITERS = 4
CX = 128
NX = 512
NY = 1024


def draw_data(key, part):
    blocks = NX // CX

    def one_block(index):
        sub_key = jax.random.fold_in(key, index)
        noise = jax.random.normal(sub_key, (V, CX, NY), jnp.float32)
        mixed = noise + 0.5 * jnp.roll(noise, 1, 0) + 0.3 * jnp.roll(noise, 5, 0)
        position = (index * CX + jnp.arange(CX)).astype(jnp.float32) / max(NX - 1, 1)
        ramp = 1.0 + 2.0 * position
        return (mixed * ramp[None, :, None]).astype(jnp.bfloat16)
    stacked = lax.map(one_block, jnp.arange(blocks, dtype=jnp.int32))
    return jnp.transpose(stacked, (1, 0, 2, 3)).reshape(V, NX, NY)


def normal_values(stream_key, dims, deviation, most, held_as=jnp.bfloat16):
    array = deviation * jax.random.normal(stream_key, dims, jnp.float32)
    return jnp.clip(array, min=-most, max=most).astype(held_as)


def setup_inputs(seed: int = 0) -> dict:
    splits = jax.random.split(jax.random.key(seed), 5)
    data = draw_data(jax.random.fold_in(splits[4], 71), 0)
    inv_scale = jnp.clip(jnp.exp(jax.random.uniform(splits[1], (V,), jnp.float32, math.log(0.1), math.log(1.0))), 0.1, 1.0)
    start = normal_values(splits[2], (V, KMAX), 1.0, 6.0, jnp.float32)
    rank = jax.random.randint(splits[3], (1,), KMAX - KMAX // 4, KMAX + 1).astype(jnp.int32)
    return {"data": data, "inv_scale": inv_scale, "start": start, "rank": rank}


def reference(data, inv_scale, start, rank):
    blocks = NX // CX

    def block_gram(index):
        piece = lax.dynamic_slice_in_dim(data, (index * CX).astype(jnp.int32), CX, 1).reshape(V, CX * NY)
        return lax.dot_general(piece.astype(jnp.float32), piece.astype(jnp.float32), (((1,), (1,)), ((), ())), preferred_element_type=jnp.float32)
    gram = jnp.sum(lax.map(block_gram, jnp.arange(blocks, dtype=jnp.int32)), axis=0)
    weighted = inv_scale[:, None] * gram * inv_scale[None, :]
    basis = start
    for turn in range(ITERS):
        image = jnp.dot(weighted, basis, precision=lax.Precision.HIGHEST)
        inner = jnp.dot(image.T, image, precision=lax.Precision.HIGHEST)
        lower = jnp.linalg.cholesky(inner)
        basis = lax.linalg.triangular_solve(lower, image, left_side=False, lower=True, transpose_a=True)
    keep = (jnp.arange(KMAX, dtype=jnp.int32) < rank[0]).astype(jnp.float32)
    factor = basis * keep[None, :]
    scaled_factor = (inv_scale[:, None] * factor).astype(jnp.bfloat16)

    def block_core(index):
        piece = lax.dynamic_slice_in_dim(data, (index * CX).astype(jnp.int32), CX, 1).reshape(V, CX * NY)
        product = lax.dot_general(scaled_factor.astype(jnp.float32), piece.astype(jnp.float32), (((0,), (0,)), ((), ())), preferred_element_type=jnp.float32)
        return product.astype(jnp.bfloat16).reshape(KMAX, CX, NY)
    stacked = lax.map(block_core, jnp.arange(blocks, dtype=jnp.int32))
    core = jnp.transpose(stacked, (1, 0, 2, 3)).reshape(KMAX, NX, NY)
    return (core, factor)
```

```python
import functools

import jax
import jax.numpy as jnp
from jax import lax
from jax.experimental import pallas as pl
from jax.experimental.pallas import tpu as pltpu
from jax.sharding import PartitionSpec as P

ITERS = 4
GROUP = 16
MESH = pl.DeviceIdType.MESH
HIGHEST = lax.Precision.HIGHEST
NT = (((1,), (1,)), ((), ()))


def gram_kernel(nx, ny, data_hbm, out_ref, slab, part, recv, mid, full,
                load_sem, send1, recv1, send2, recv2, send3, recv3):
    variables, rows, columns = data_hbm.shape
    chunks = rows // GROUP
    height = variables // ny
    me_x = lax.axis_index("gx")
    me_y = lax.axis_index("gy")

    def load(c):
        return pltpu.make_async_copy(
            data_hbm.at[:, pl.ds(c * GROUP, GROUP), :], slab.at[c], load_sem.at[c])

    for c in range(chunks):
        load(c).start()
    barrier = pltpu.get_barrier_semaphore()
    for p in range(1, ny):
        pl.semaphore_signal(barrier, inc=1, device_id=(me_x, lax.rem(me_y + p, ny)), device_id_type=MESH)
    for p in range(1, nx):
        pl.semaphore_signal(barrier, inc=1, device_id=(lax.rem(me_x + p, nx), me_y), device_id_type=MESH)

    gram = jnp.zeros((variables, variables), jnp.float32)
    for c in range(chunks):
        load(c).wait()
        turned = jnp.swapaxes(slab[c], 0, 1)
        for i in range(0, GROUP, 2):
            pair = jnp.concatenate([turned[i], turned[i + 1]], axis=1)
            gram = gram + lax.dot_general(pair, pair, NT, preferred_element_type=jnp.float32)
    for p in range(ny):
        part[p] = gram[p * height:(p + 1) * height, :]
    pl.semaphore_wait(barrier, nx + ny - 2)

    def scatter(p):
        dst = lax.rem(me_y + p, ny)
        return pltpu.make_async_remote_copy(
            src_ref=part.at[dst], dst_ref=recv.at[p - 1],
            send_sem=send1.at[p - 1], recv_sem=recv1.at[p - 1],
            device_id=(me_x, dst), device_id_type=MESH)

    for p in range(1, ny):
        scatter(p).start()
    total = part[me_y]
    for p in range(1, ny):
        scatter(p).wait_recv()
        total = total + recv[p - 1]
    mid[me_x] = total

    def exchange(p):
        return pltpu.make_async_remote_copy(
            src_ref=mid.at[me_x], dst_ref=mid.at[me_x],
            send_sem=send2.at[p - 1], recv_sem=recv2.at[p - 1],
            device_id=(lax.rem(me_x + p, nx), me_y), device_id_type=MESH)

    for p in range(1, nx):
        exchange(p).start()
    for p in range(1, nx):
        exchange(p).wait_recv()
    total = mid[0]
    for s in range(1, nx):
        total = total + mid[s]
    full[me_y] = total

    def gather(p):
        return pltpu.make_async_remote_copy(
            src_ref=full.at[me_y], dst_ref=full.at[me_y],
            send_sem=send3.at[p - 1], recv_sem=recv3.at[p - 1],
            device_id=(me_x, lax.rem(me_y + p, ny)), device_id_type=MESH)

    for p in range(1, ny):
        gather(p).start()
    for p in range(1, ny):
        gather(p).wait_recv()
    for p in range(ny):
        out_ref[p * height:(p + 1) * height, :] = full[p]
    for p in range(1, ny):
        scatter(p).wait_send()
        gather(p).wait_send()
    for p in range(1, nx):
        exchange(p).wait_send()


def summed_gram(mesh, data):
    nx, ny = mesh.shape["gx"], mesh.shape["gy"]
    variables, rows, columns = data.shape
    chunks = rows // GROUP
    height = variables // ny
    dma = pltpu.SemaphoreType.DMA
    return pl.pallas_call(
        functools.partial(gram_kernel, nx, ny),
        out_shape=jax.ShapeDtypeStruct((variables, variables), jnp.float32),
        in_specs=[pl.BlockSpec(memory_space=pl.ANY)],
        out_specs=pl.BlockSpec(memory_space=pltpu.VMEM),
        scratch_shapes=[
            pltpu.VMEM((chunks, variables, GROUP, columns), data.dtype),
            pltpu.VMEM((ny, height, variables), jnp.float32),
            pltpu.VMEM((ny - 1, height, variables), jnp.float32),
            pltpu.VMEM((nx, height, variables), jnp.float32),
            pltpu.VMEM((ny, height, variables), jnp.float32),
            dma((chunks,)),
            dma((ny - 1,)), dma((ny - 1,)),
            dma((nx - 1,)), dma((nx - 1,)),
            dma((ny - 1,)), dma((ny - 1,)),
        ],
        compiler_params=pltpu.CompilerParams(collective_id=0, has_side_effects=True),
        name="gram",
    )(data)


def orthonormal(image):
    count, lanes = image.shape
    inner = lax.dot_general(image, image, NT, precision=HIGHEST, preferred_element_type=jnp.float32)
    blocks = count // 8
    sub = lax.broadcasted_iota(jnp.int32, (8, lanes), 0)
    cols = []
    for k in range(count):
        wide = jnp.broadcast_to(inner[:, k:k + 1], (count, lanes))
        cols.append([wide[8 * b:8 * b + 8] for b in range(blocks)])
    img = [image[8 * b:8 * b + 8] for b in range(blocks)]

    def spread(block, row):
        return jnp.broadcast_to(block[row:row + 1, :], (8, lanes))

    for k in range(count):
        kb, kr = divmod(k, 8)
        col = cols[k]
        pivot = spread(col[kb], kr)
        inverse = 1.0 / pivot
        scale = lax.rsqrt(pivot)
        row = spread(img[kb], kr)
        low = {}
        for b in range(kb, blocks):
            value = col[b] * inverse
            if b == kb:
                value = jnp.where(sub > kr, value, 0.0)
            low[b] = value
        for j in range(k + 1, count):
            jb, jr = divmod(j, 8)
            factor = spread(col[jb], jr)
            for b in range(jb, blocks):
                cols[j][b] = cols[j][b] - low[b] * factor
        for b in range(kb, blocks):
            img[b] = img[b] - low[b] * row
        img[kb] = img[kb] * jnp.where(sub == kr, scale, 1.0)
    return jnp.concatenate(img, axis=0)


def project_kernel(rank_ref, gram_ref, scale_ref, start_ref, data_hbm, core_hbm, factor_ref,
                   slab, done, load_sem, store_sem):
    variables, rows, columns = data_hbm.shape
    count = start_ref.shape[1]
    chunks = rows // GROUP

    def load(c):
        return pltpu.make_async_copy(
            data_hbm.at[:, pl.ds(c * GROUP, GROUP), :], slab.at[c], load_sem.at[c])

    def store(c):
        return pltpu.make_async_copy(
            done.at[c], core_hbm.at[:, pl.ds(c * GROUP, GROUP), :], store_sem.at[c])

    for c in range(chunks):
        load(c).start()
    scale_row = jnp.broadcast_to(scale_ref[...], (variables, variables))
    weighted = scale_row.T * gram_ref[...] * scale_row
    basis = start_ref[...].T

    def turn(_, basis):
        image = jnp.dot(basis, weighted, precision=HIGHEST, preferred_element_type=jnp.float32)
        return orthonormal(image)

    basis = lax.fori_loop(0, ITERS, turn, basis)
    kept = lax.broadcasted_iota(jnp.int32, basis.shape, 0) < rank_ref[0]
    factor = jnp.where(kept, basis, 0.0)
    factor_ref[...] = factor.T
    scaled = (scale_row[:count] * factor).astype(jnp.bfloat16)

    tall, long = count * GROUP, variables * GROUP
    pick_k = (lax.broadcasted_iota(jnp.int32, (tall, count), 0) // GROUP
              == lax.broadcasted_iota(jnp.int32, (tall, count), 1)).astype(jnp.bfloat16)
    pick_v = (lax.broadcasted_iota(jnp.int32, (variables, long), 1) // GROUP
              == lax.broadcasted_iota(jnp.int32, (variables, long), 0)).astype(jnp.bfloat16)
    repeated = jnp.dot(pick_k, scaled, preferred_element_type=jnp.float32).astype(jnp.bfloat16)
    spread = jnp.dot(repeated, pick_v, preferred_element_type=jnp.float32)
    same = (lax.broadcasted_iota(jnp.int32, (tall, long), 0) % GROUP
            == lax.broadcasted_iota(jnp.int32, (tall, long), 1) % GROUP)
    wide = jnp.where(same, spread, 0.0).astype(jnp.bfloat16)
    for c in range(0, chunks, 2):
        load(c).wait()
        load(c + 1).wait()
        pair = jnp.concatenate([slab[c].reshape(long, columns), slab[c + 1].reshape(long, columns)], axis=1)
        product = jnp.dot(wide, pair, preferred_element_type=jnp.float32).astype(jnp.bfloat16)
        for h in range(2):
            done[c + h] = product[:, h * columns:(h + 1) * columns].reshape(count, GROUP, columns)
            store(c + h).start()
    for c in range(chunks):
        store(c).wait()


def project(rank, gram, inv_scale, start, data):
    variables, rows, columns = data.shape
    count = start.shape[1]
    chunks = rows // GROUP
    vmem = pl.BlockSpec(memory_space=pltpu.VMEM)
    return pl.pallas_call(
        project_kernel,
        out_shape=(
            jax.ShapeDtypeStruct((count, rows, columns), data.dtype),
            jax.ShapeDtypeStruct((variables, count), jnp.float32),
        ),
        in_specs=[pl.BlockSpec(memory_space=pltpu.SMEM), vmem, vmem, vmem,
                  pl.BlockSpec(memory_space=pl.ANY)],
        out_specs=(pl.BlockSpec(memory_space=pl.ANY), vmem),
        scratch_shapes=[
            pltpu.VMEM((chunks, variables, GROUP, columns), data.dtype),
            pltpu.VMEM((chunks, count, GROUP, columns), data.dtype),
            pltpu.SemaphoreType.DMA((chunks,)),
            pltpu.SemaphoreType.DMA((chunks,)),
        ],
        name="project",
    )(rank, gram, inv_scale.reshape(1, variables), start, data)


def solution(mesh):
    def body(data, inv_scale, start, rank):
        gram = summed_gram(mesh, data)
        return project(rank, gram, inv_scale, start, data)

    in_specs = (P(None, "gx", "gy"), P(), P(), P())
    out_specs = (P(None, "gx", "gy"), P())
    return jax.shard_map(body, mesh=mesh, in_specs=in_specs, out_specs=out_specs, check_vma=False)
```

```python
import functools

import jax
import jax.numpy as jnp
from jax import lax
from jax.experimental import pallas as pl
from jax.experimental.pallas import tpu as pltpu
from jax.sharding import PartitionSpec as P

ITERS = 4
GROUP = 16
MESH = pl.DeviceIdType.MESH
HIGHEST = lax.Precision.HIGHEST
NT = (((1,), (1,)), ((), ()))


def gram_kernel(nx, ny, data_hbm, out_ref, turned_hbm, slab, turned, part, recv, mid, full,
                load_sem, keep_sem, send1, recv1, send2, recv2, send3, recv3):
    variables, rows, columns = data_hbm.shape
    chunks = rows // GROUP
    height = variables // ny
    me_x = lax.axis_index("gx")
    me_y = lax.axis_index("gy")

    def load(c):
        return pltpu.make_async_copy(
            data_hbm.at[:, pl.ds(c * GROUP, GROUP), :], slab.at[c], load_sem.at[c])

    def keep(c):
        return pltpu.make_async_copy(
            turned.at[c], turned_hbm.at[pl.ds(c * GROUP, GROUP)], keep_sem.at[c])

    for c in range(chunks):
        load(c).start()
    barrier = pltpu.get_barrier_semaphore()
    for p in range(1, ny):
        pl.semaphore_signal(barrier, inc=1, device_id=(me_x, lax.rem(me_y + p, ny)), device_id_type=MESH)
    for p in range(1, nx):
        pl.semaphore_signal(barrier, inc=1, device_id=(lax.rem(me_x + p, nx), me_y), device_id_type=MESH)

    gram = jnp.zeros((variables, variables), jnp.float32)
    for c in range(chunks):
        load(c).wait()
        block = jnp.swapaxes(slab[c], 0, 1)
        turned[c] = block
        for i in range(0, GROUP, 2):
            pair = jnp.concatenate([block[i], block[i + 1]], axis=1)
            gram = gram + lax.dot_general(pair, pair, NT, preferred_element_type=jnp.float32)
    for p in range(ny):
        part[p] = gram[p * height:(p + 1) * height, :]
    pl.semaphore_wait(barrier, nx + ny - 2)

    def scatter(p):
        dst = lax.rem(me_y + p, ny)
        return pltpu.make_async_remote_copy(
            src_ref=part.at[dst], dst_ref=recv.at[p - 1],
            send_sem=send1.at[p - 1], recv_sem=recv1.at[p - 1],
            device_id=(me_x, dst), device_id_type=MESH)

    for p in range(1, ny):
        scatter(p).start()
    for c in range(chunks):
        keep(c).start()
    total = part[me_y]
    for p in range(1, ny):
        scatter(p).wait_recv()
        total = total + recv[p - 1]
    mid[me_x] = total

    def exchange(p):
        return pltpu.make_async_remote_copy(
            src_ref=mid.at[me_x], dst_ref=mid.at[me_x],
            send_sem=send2.at[p - 1], recv_sem=recv2.at[p - 1],
            device_id=(lax.rem(me_x + p, nx), me_y), device_id_type=MESH)

    for p in range(1, nx):
        exchange(p).start()
    for p in range(1, nx):
        exchange(p).wait_recv()
    total = mid[0]
    for s in range(1, nx):
        total = total + mid[s]
    full[me_y] = total

    def gather(p):
        return pltpu.make_async_remote_copy(
            src_ref=full.at[me_y], dst_ref=full.at[me_y],
            send_sem=send3.at[p - 1], recv_sem=recv3.at[p - 1],
            device_id=(me_x, lax.rem(me_y + p, ny)), device_id_type=MESH)

    for p in range(1, ny):
        gather(p).start()
    for p in range(1, ny):
        gather(p).wait_recv()
    for p in range(ny):
        out_ref[p * height:(p + 1) * height, :] = full[p]
    for p in range(1, ny):
        scatter(p).wait_send()
        gather(p).wait_send()
    for p in range(1, nx):
        exchange(p).wait_send()
    for c in range(chunks):
        keep(c).wait()


def summed_gram(mesh, data):
    nx, ny = mesh.shape["gx"], mesh.shape["gy"]
    variables, rows, columns = data.shape
    chunks = rows // GROUP
    height = variables // ny
    dma = pltpu.SemaphoreType.DMA
    return pl.pallas_call(
        functools.partial(gram_kernel, nx, ny),
        out_shape=(
            jax.ShapeDtypeStruct((variables, variables), jnp.float32),
            jax.ShapeDtypeStruct((rows, variables, columns), data.dtype),
        ),
        in_specs=[pl.BlockSpec(memory_space=pl.ANY)],
        out_specs=(pl.BlockSpec(memory_space=pltpu.VMEM), pl.BlockSpec(memory_space=pl.ANY)),
        scratch_shapes=[
            pltpu.VMEM((chunks, variables, GROUP, columns), data.dtype),
            pltpu.VMEM((chunks, GROUP, variables, columns), data.dtype),
            pltpu.VMEM((ny, height, variables), jnp.float32),
            pltpu.VMEM((ny - 1, height, variables), jnp.float32),
            pltpu.VMEM((nx, height, variables), jnp.float32),
            pltpu.VMEM((ny, height, variables), jnp.float32),
            dma((chunks,)), dma((chunks,)),
            dma((ny - 1,)), dma((ny - 1,)),
            dma((nx - 1,)), dma((nx - 1,)),
            dma((ny - 1,)), dma((ny - 1,)),
        ],
        compiler_params=pltpu.CompilerParams(collective_id=0, has_side_effects=True),
        name="gram",
    )(data)


def orthonormal(image):
    count, lanes = image.shape
    inner = lax.dot_general(image, image, NT, precision=HIGHEST, preferred_element_type=jnp.float32)
    blocks = count // 8
    sub = lax.broadcasted_iota(jnp.int32, (8, lanes), 0)
    cols = []
    for k in range(count):
        wide = jnp.broadcast_to(inner[:, k:k + 1], (count, lanes))
        cols.append([wide[8 * b:8 * b + 8] for b in range(blocks)])
    img = [image[8 * b:8 * b + 8] for b in range(blocks)]

    def spread(block, row):
        return jnp.broadcast_to(block[row:row + 1, :], (8, lanes))

    for k in range(count):
        kb, kr = divmod(k, 8)
        col = cols[k]
        pivot = spread(col[kb], kr)
        inverse = 1.0 / pivot
        scale = lax.rsqrt(pivot)
        row = spread(img[kb], kr)
        low = {}
        for b in range(kb, blocks):
            value = col[b] * inverse
            if b == kb:
                value = jnp.where(sub > kr, value, 0.0)
            low[b] = value
        for j in range(k + 1, count):
            jb, jr = divmod(j, 8)
            factor = spread(col[jb], jr)
            for b in range(jb, blocks):
                cols[j][b] = cols[j][b] - low[b] * factor
        for b in range(kb, blocks):
            img[b] = img[b] - low[b] * row
        img[kb] = img[kb] * jnp.where(sub == kr, scale, 1.0)
    return jnp.concatenate(img, axis=0)


def project_kernel(rank_ref, gram_ref, scale_ref, start_ref, turned_hbm, core_hbm, factor_ref,
                   slab, done, load_sem, store_sem):
    rows, variables, columns = turned_hbm.shape
    count = start_ref.shape[0]
    chunks = rows // GROUP

    def load(c):
        return pltpu.make_async_copy(
            turned_hbm.at[pl.ds(c * GROUP, GROUP)], slab.at[c], load_sem.at[c])

    def store(c):
        return pltpu.make_async_copy(
            done.at[c], core_hbm.at[:, pl.ds(c * GROUP, GROUP), :], store_sem.at[c])

    for c in range(chunks):
        load(c).start()
    scale_row = jnp.broadcast_to(scale_ref[...], (variables, variables))
    weighted = scale_row.T * gram_ref[...] * scale_row
    basis = start_ref[...]

    def turn(_, basis):
        image = jnp.dot(basis, weighted, precision=HIGHEST, preferred_element_type=jnp.float32)
        return orthonormal(image)

    basis = lax.fori_loop(0, ITERS, turn, basis)
    kept = lax.broadcasted_iota(jnp.int32, basis.shape, 0) < rank_ref[0]
    factor = jnp.where(kept, basis, 0.0)
    factor_ref[...] = factor
    scaled = (scale_row[:count] * factor).astype(jnp.bfloat16)

    for c in range(chunks):
        load(c).wait()
        planes = []
        for i in range(0, GROUP, 2):
            pair = jnp.concatenate([slab[c, i], slab[c, i + 1]], axis=1)
            product = jnp.dot(scaled, pair, preferred_element_type=jnp.float32).astype(jnp.bfloat16)
            planes += [product[:, :columns], product[:, columns:]]
        done[c] = jnp.swapaxes(jnp.stack(planes), 0, 1)
        store(c).start()
    for c in range(chunks):
        store(c).wait()


def project(rank, gram, inv_scale, start, data):
    rows, variables, columns = data.shape
    count = start.shape[1]
    chunks = rows // GROUP
    vmem = pl.BlockSpec(memory_space=pltpu.VMEM)
    core, turned = pl.pallas_call(
        project_kernel,
        out_shape=(
            jax.ShapeDtypeStruct((count, rows, columns), data.dtype),
            jax.ShapeDtypeStruct((count, variables), jnp.float32),
        ),
        in_specs=[pl.BlockSpec(memory_space=pltpu.SMEM), vmem, vmem, vmem,
                  pl.BlockSpec(memory_space=pl.ANY)],
        out_specs=(pl.BlockSpec(memory_space=pl.ANY), vmem),
        scratch_shapes=[
            pltpu.VMEM((chunks, GROUP, variables, columns), data.dtype),
            pltpu.VMEM((chunks, count, GROUP, columns), data.dtype),
            pltpu.SemaphoreType.DMA((chunks,)),
            pltpu.SemaphoreType.DMA((chunks,)),
        ],
        name="project",
    )(rank, gram, inv_scale.reshape(1, variables), start.T, data)
    return core, turned.T


def solution(mesh):
    def body(data, inv_scale, start, rank):
        gram, turned = summed_gram(mesh, data)
        return project(rank, gram, inv_scale, start, turned)

    in_specs = (P(None, "gx", "gy"), P(), P(), P())
    out_specs = (P(None, "gx", "gy"), P())
    return jax.shard_map(body, mesh=mesh, in_specs=in_specs, out_specs=out_specs, check_vma=False)
```

```python
import functools

import jax
import jax.numpy as jnp
from jax import lax
from jax.experimental import pallas as pl
from jax.experimental.pallas import tpu as pltpu
from jax.sharding import PartitionSpec as P

ITERS = 4
GROUP = 16
MESH = pl.DeviceIdType.MESH
HIGHEST = lax.Precision.HIGHEST
NT = (((1,), (1,)), ((), ()))


def gram_kernel(nx, ny, data_hbm, out_ref, turned_hbm, slab, turned, part, recv, mid, full,
                load_sem, keep_sem, send1, recv1, send2, recv2, send3, recv3):
    variables, rows, columns = data_hbm.shape
    chunks = rows // GROUP
    height = variables // ny
    me_x = lax.axis_index("gx")
    me_y = lax.axis_index("gy")

    def load(c):
        return pltpu.make_async_copy(
            data_hbm.at[:, pl.ds(c * GROUP, GROUP), :], slab.at[c], load_sem.at[c])

    def keep(c):
        return pltpu.make_async_copy(
            turned.at[c], turned_hbm.at[pl.ds(c * GROUP, GROUP)], keep_sem.at[c])

    for c in range(chunks):
        load(c).start()
    barrier = pltpu.get_barrier_semaphore()
    for p in range(1, ny):
        pl.semaphore_signal(barrier, inc=1, device_id=(me_x, lax.rem(me_y + p, ny)), device_id_type=MESH)
    for p in range(1, nx):
        pl.semaphore_signal(barrier, inc=1, device_id=(lax.rem(me_x + p, nx), me_y), device_id_type=MESH)

    gram = jnp.zeros((variables, variables), jnp.float32)
    for c in range(chunks):
        load(c).wait()
        block = jnp.swapaxes(slab[c], 0, 1)
        turned[c] = block
        for i in range(0, GROUP, 2):
            pair = jnp.concatenate([block[i], block[i + 1]], axis=1)
            gram = gram + lax.dot_general(pair, pair, NT, preferred_element_type=jnp.float32)
    for p in range(ny):
        part[p] = gram[p * height:(p + 1) * height, :]
    pl.semaphore_wait(barrier, nx + ny - 2)

    def scatter(p):
        dst = lax.rem(me_y + p, ny)
        return pltpu.make_async_remote_copy(
            src_ref=part.at[dst], dst_ref=recv.at[p - 1],
            send_sem=send1.at[p - 1], recv_sem=recv1.at[p - 1],
            device_id=(me_x, dst), device_id_type=MESH)

    for p in range(1, ny):
        scatter(p).start()
    total = part[me_y]
    for p in range(1, ny):
        scatter(p).wait_recv()
        total = total + recv[p - 1]
    mid[me_x] = total

    def exchange(p):
        return pltpu.make_async_remote_copy(
            src_ref=mid.at[me_x], dst_ref=mid.at[me_x],
            send_sem=send2.at[p - 1], recv_sem=recv2.at[p - 1],
            device_id=(lax.rem(me_x + p, nx), me_y), device_id_type=MESH)

    for p in range(1, nx):
        exchange(p).start()
    for p in range(1, nx):
        exchange(p).wait_recv()
    total = mid[0]
    for s in range(1, nx):
        total = total + mid[s]
    full[me_y] = total

    def gather(p):
        return pltpu.make_async_remote_copy(
            src_ref=full.at[me_y], dst_ref=full.at[me_y],
            send_sem=send3.at[p - 1], recv_sem=recv3.at[p - 1],
            device_id=(me_x, lax.rem(me_y + p, ny)), device_id_type=MESH)

    for p in range(1, ny):
        gather(p).start()
    for c in range(chunks):
        keep(c).start()
    for p in range(1, ny):
        gather(p).wait_recv()
    for p in range(ny):
        out_ref[p * height:(p + 1) * height, :] = full[p]
    for p in range(1, ny):
        scatter(p).wait_send()
        gather(p).wait_send()
    for p in range(1, nx):
        exchange(p).wait_send()
    for c in range(chunks):
        keep(c).wait()


def summed_gram(mesh, data):
    nx, ny = mesh.shape["gx"], mesh.shape["gy"]
    variables, rows, columns = data.shape
    chunks = rows // GROUP
    height = variables // ny
    dma = pltpu.SemaphoreType.DMA
    return pl.pallas_call(
        functools.partial(gram_kernel, nx, ny),
        out_shape=(
            jax.ShapeDtypeStruct((variables, variables), jnp.float32),
            jax.ShapeDtypeStruct((rows, variables, columns), data.dtype),
        ),
        in_specs=[pl.BlockSpec(memory_space=pl.ANY)],
        out_specs=(pl.BlockSpec(memory_space=pltpu.VMEM), pl.BlockSpec(memory_space=pl.ANY)),
        scratch_shapes=[
            pltpu.VMEM((chunks, variables, GROUP, columns), data.dtype),
            pltpu.VMEM((chunks, GROUP, variables, columns), data.dtype),
            pltpu.VMEM((ny, height, variables), jnp.float32),
            pltpu.VMEM((ny - 1, height, variables), jnp.float32),
            pltpu.VMEM((nx, height, variables), jnp.float32),
            pltpu.VMEM((ny, height, variables), jnp.float32),
            dma((chunks,)), dma((chunks,)),
            dma((ny - 1,)), dma((ny - 1,)),
            dma((nx - 1,)), dma((nx - 1,)),
            dma((ny - 1,)), dma((ny - 1,)),
        ],
        compiler_params=pltpu.CompilerParams(collective_id=0, has_side_effects=True),
        name="gram",
    )(data)


def orthonormal(image):
    count, lanes = image.shape
    inner = lax.dot_general(image, image, NT, precision=HIGHEST, preferred_element_type=jnp.float32)
    blocks = count // 8
    sub = lax.broadcasted_iota(jnp.int32, (8, lanes), 0)
    cols = []
    for k in range(count):
        wide = jnp.broadcast_to(inner[:, k:k + 1], (count, lanes))
        cols.append([wide[8 * b:8 * b + 8] for b in range(blocks)])
    img = [image[8 * b:8 * b + 8] for b in range(blocks)]

    def spread(block, row):
        return jnp.broadcast_to(block[row:row + 1, :], (8, lanes))

    for k in range(count):
        kb, kr = divmod(k, 8)
        col = cols[k]
        pivot = spread(col[kb], kr)
        inverse = 1.0 / pivot
        scale = lax.rsqrt(pivot)
        row = spread(img[kb], kr)
        low = {}
        for b in range(kb, blocks):
            value = col[b] * inverse
            if b == kb:
                value = jnp.where(sub > kr, value, 0.0)
            low[b] = value
        for j in range(k + 1, count):
            jb, jr = divmod(j, 8)
            factor = spread(col[jb], jr)
            for b in range(jb, blocks):
                cols[j][b] = cols[j][b] - low[b] * factor
        for b in range(kb, blocks):
            img[b] = img[b] - low[b] * row
        img[kb] = img[kb] * jnp.where(sub == kr, scale, 1.0)
    return jnp.concatenate(img, axis=0)


def project_kernel(rank_ref, gram_ref, scale_ref, start_ref, turned_hbm, core_hbm, factor_ref,
                   slab, done, load_sem, store_sem):
    rows, variables, columns = turned_hbm.shape
    count = start_ref.shape[0]
    chunks = rows // GROUP

    def load(c):
        return pltpu.make_async_copy(
            turned_hbm.at[pl.ds(c * GROUP, GROUP)], slab.at[c], load_sem.at[c])

    def store(c):
        return pltpu.make_async_copy(
            done.at[c], core_hbm.at[:, pl.ds(c * GROUP, GROUP), :], store_sem.at[c])

    for c in range(chunks):
        load(c).start()
    scale_row = jnp.broadcast_to(scale_ref[...], (variables, variables))
    weighted = scale_row.T * gram_ref[...] * scale_row
    basis = start_ref[...]

    def turn(_, basis):
        image = jnp.dot(basis, weighted, precision=HIGHEST, preferred_element_type=jnp.float32)
        return orthonormal(image)

    basis = lax.fori_loop(0, ITERS, turn, basis)
    kept = lax.broadcasted_iota(jnp.int32, basis.shape, 0) < rank_ref[0]
    factor = jnp.where(kept, basis, 0.0)
    factor_ref[...] = factor
    scaled = (scale_row[:count] * factor).astype(jnp.bfloat16)

    for c in range(chunks):
        load(c).wait()
        planes = []
        for i in range(0, GROUP, 2):
            pair = jnp.concatenate([slab[c, i], slab[c, i + 1]], axis=1)
            product = jnp.dot(scaled, pair, preferred_element_type=jnp.float32).astype(jnp.bfloat16)
            planes += [product[:, :columns], product[:, columns:]]
        done[c] = jnp.swapaxes(jnp.stack(planes), 0, 1)
        store(c).start()
    for c in range(chunks):
        store(c).wait()


def project(rank, gram, inv_scale, start, data):
    rows, variables, columns = data.shape
    count = start.shape[1]
    chunks = rows // GROUP
    vmem = pl.BlockSpec(memory_space=pltpu.VMEM)
    core, turned = pl.pallas_call(
        project_kernel,
        out_shape=(
            jax.ShapeDtypeStruct((count, rows, columns), data.dtype),
            jax.ShapeDtypeStruct((count, variables), jnp.float32),
        ),
        in_specs=[pl.BlockSpec(memory_space=pltpu.SMEM), vmem, vmem, vmem,
                  pl.BlockSpec(memory_space=pl.ANY)],
        out_specs=(pl.BlockSpec(memory_space=pl.ANY), vmem),
        scratch_shapes=[
            pltpu.VMEM((chunks, GROUP, variables, columns), data.dtype),
            pltpu.VMEM((chunks, count, GROUP, columns), data.dtype),
            pltpu.SemaphoreType.DMA((chunks,)),
            pltpu.SemaphoreType.DMA((chunks,)),
        ],
        name="project",
    )(rank, gram, inv_scale.reshape(1, variables), start.T, data)
    return core, turned.T


def solution(mesh):
    def body(data, inv_scale, start, rank):
        gram, turned = summed_gram(mesh, data)
        return project(rank, gram, inv_scale, start, turned)

    in_specs = (P(None, "gx", "gy"), P(), P(), P())
    out_specs = (P(None, "gx", "gy"), P())
    return jax.shard_map(body, mesh=mesh, in_specs=in_specs, out_specs=out_specs, check_vma=False)
```
